512 devices in a mesh: tile: 32 (over x, y), depth: 16 (over z, core).
Axes of the slice: x: 4, y: 8, z: 8, core: 2. Of those that a mesh axis runs over, the one named last changes fastest.
Arguments:
- coefficients: float32 [8, 16, 32, 128, 128], P(None, 'depth', 'tile'), may hold values from -24 to 24
- keep_count: int32 [16, 32, 128, 128], P('depth', 'tile'), may hold values from 1 to 8, as said below
- view_flip: int32 [32], P('tile'), may hold values from 0 to 1
Outputs:
- image: float32 [4, 512, 512], P(None, 'tile', 'depth')
The draws below stay inside these ranges and needn't reach their ends.
Inputs may be any that keep to these rules, and one draw needn't show every extreme that they name: `keep_count`: along the block rows, blocks 2 j and 2 j + 1 of every brick and block column retain 8 + 1 slots together.
All inputs are finite; a program needn't handle non-finite values.
Results may differ from the reference program's by a relative error of at most 0.0003.
Values sent between devices are 32-bit elements; how exact they have to be, the bound alone decides.
A program may use at most 64 MiB of HBM per device.

```python
import math
import jax
import jax.numpy as jnp
import numpy as np
from jax import lax

KMAX = 8
GY = 512
GX = 512
GZ = 2048
TXB = 4
GXB = 128
GYB = 128
N_TILE = 32
N_DEPTH = 16


def draw_keep_count(key, part):
    first = jax.random.randint(jax.random.fold_in(key, 11), (N_DEPTH, N_TILE, GXB, GYB // 2), 1, KMAX + 1)
    second = KMAX + 1 - first
    return jnp.stack([first, second], axis=-1).reshape(N_DEPTH, N_TILE, GXB, GYB).astype(jnp.int32)


def set_ends(values, key, low, top_value):
    dims = values.shape
    place = [jax.random.randint(jax.random.fold_in(key, axis), (), 0, dims[axis]) for axis in range(len(dims))]
    values = values.at[tuple(place)].set(low)
    longest = dims.index(max(dims))
    place[longest] = (place[longest] + 1) % dims[longest]
    return values.at[tuple(place)].set(top_value)


def levels(own_key, shape, shards, smallest, top_value):
    loudness = 1.0
    for dim, blocks in shards:
        draws = jax.random.uniform(jax.random.fold_in(jax.random.fold_in(own_key, 6), dim), (blocks,), jnp.float32, smallest / len(shards), top_value / len(shards))
        loudness = loudness * jnp.repeat(jnp.exp(draws), shape[dim] // blocks).reshape((-1,) + (1,) * (len(shape) - 1 - dim))
    return loudness


def gaussian(key, dims, scale, most, cuts=(), kind=jnp.bfloat16):
    array = jax.random.normal(key, dims, jnp.float32) * scale
    if len(cuts) > 0:
        array = levels(key, dims, cuts, -0.22, 0.18) * array
    return jnp.clip(array, min=-most, max=most).astype(kind)


def setup_inputs(seed: int = 0) -> dict:
    arg_keys = jax.random.split(jax.random.key(seed), 4)
    coefficients = gaussian(arg_keys[0], (KMAX, N_DEPTH, N_TILE, GXB, GYB), 4.0, 24.0, ((1, 16), (2, 32)), jnp.float32)
    keep_count = draw_keep_count(jax.random.fold_in(arg_keys[3], 71), 0)
    view_flip = set_ends(jax.random.randint(arg_keys[2], (N_TILE,), 0, 2), jax.random.fold_in(arg_keys[2], 1), 0, 1).astype(jnp.int32)
    return {"coefficients": coefficients, "keep_count": keep_count, "view_flip": view_flip}


slot_frequencies = ((0, 0, 0), (0, 0, 1), (0, 1, 0), (1, 0, 0), (0, 0, 2), (0, 1, 1), (0, 2, 0), (1, 0, 1))

def cosine_rows():
    result = np.zeros((4, 4))
    for frequency in range(4):
        factor = 0.5 if frequency == 0 else math.sqrt(0.5)
        for position in range(4):
            result[frequency, position] = factor * math.cos(math.pi * (2 * position + 1) * frequency / 8.0)
    return result

def basis_matrix(slot_count):
    rows_table = cosine_rows()
    result = np.zeros((4, 4, 4, slot_count))
    for slot_index in range(slot_count):
        freq_z, freq_x, freq_y = slot_frequencies[slot_index]
        result[:, :, :, slot_index] = rows_table[freq_z][:, None, None] * rows_table[freq_x][None, :, None] * rows_table[freq_y][None, None, :]
    return jnp.asarray(result.reshape(64, slot_count), dtype=jnp.float32)

def render_columns(block_coef, basis_rows, flipped, sample_count):
    slot_count, zblocks, column_count = block_coef.shape
    flat_coef = block_coef.reshape(slot_count, zblocks * column_count)
    cell_values = jnp.dot(basis_rows, flat_coef, precision=lax.Precision.HIGHEST, preferred_element_type=jnp.float32)
    cell_values = cell_values.reshape(4, 16, zblocks, column_count)
    density = jnp.transpose(cell_values, (2, 0, 1, 3)).reshape(zblocks * 4, 16, column_count)
    optical = 1.5 * jax.nn.softplus(2.0 * density) / sample_count
    inclusive = jnp.cumsum(optical, axis=0)
    total_depth = inclusive[-1]
    entering = jnp.where(flipped > 0, total_depth[None] - inclusive, inclusive - optical)
    weights = jnp.exp(-entering) * -jnp.expm1(-optical)
    red_sum = lax.optimization_barrier(jnp.sum(weights * jax.nn.sigmoid(2.0 * density), axis=0))
    green_sum = lax.optimization_barrier(jnp.sum(weights * jnp.exp(-density * density), axis=0))
    blue_sum = lax.optimization_barrier(jnp.sum(weights * jax.nn.sigmoid(1.5 - density), axis=0))
    opacity = -jnp.expm1(-total_depth)
    return jnp.stack([red_sum, green_sum, blue_sum, opacity])

def to_image(layer, strip_blocks, column_blocks):
    spread = layer.reshape(4, 4, 4, strip_blocks, column_blocks)
    return jnp.transpose(spread, (0, 3, 1, 4, 2)).reshape(4, strip_blocks * 4, column_blocks * 4)

def composite(layers, flipped, layer_axis):
    clearance = 1.0 - layers[3:4]
    piece_count = layers.shape[layer_axis]
    forward = jnp.cumprod(clearance, axis=layer_axis)
    backward = jnp.flip(jnp.cumprod(jnp.flip(clearance, layer_axis), axis=layer_axis), layer_axis)
    unit_slice = jnp.ones_like(lax.slice_in_dim(clearance, 0, 1, axis=layer_axis))
    before_forward = jnp.concatenate([unit_slice, lax.slice_in_dim(forward, 0, piece_count - 1, axis=layer_axis)], axis=layer_axis)
    before_backward = jnp.concatenate([lax.slice_in_dim(backward, 1, piece_count, axis=layer_axis), unit_slice], axis=layer_axis)
    passing = jnp.where(flipped > 0, before_backward, before_forward)
    return lax.optimization_barrier(jnp.sum(passing * layers, axis=layer_axis))

def reference(coefficients, keep_count, view_flip):
    slot_index = lax.broadcasted_iota(jnp.int32, coefficients.shape, 0)
    masked = jnp.where(slot_index < keep_count[None], coefficients, jnp.float32(0.0))
    basis_rows = basis_matrix(KMAX)
    bricks = masked.reshape(KMAX, N_DEPTH, N_TILE, N_TILE, TXB, GYB)
    bricks = jnp.transpose(bricks, (3, 1, 0, 2, 4, 5)).reshape(N_TILE, N_DEPTH, KMAX, N_TILE, TXB * GYB)

    def per_tile(inputs):
        tile_bricks, flipped = inputs

        def per_brick(brick_coef):
            layer = render_columns(brick_coef, basis_rows, flipped, GZ)
            return to_image(layer, TXB, GYB)
        layers = lax.map(per_brick, tile_bricks)
        layers = jnp.moveaxis(layers, 0, 1)
        return composite(layers, flipped, 1)
    strips = lax.map(per_tile, (bricks, view_flip))
    return jnp.transpose(strips, (1, 0, 2, 3)).reshape(4, GX, GY)
```

```python
import functools
import math

import jax
import jax.numpy as jnp
from jax import lax
from jax.experimental import pallas as pl
from jax.experimental.pallas import tpu as pltpu
from jax.sharding import PartitionSpec as P

MESH = pl.DeviceIdType.MESH
LOG2E = math.log2(math.e)


def cosine(frequency, position):
    factor = 0.5 if frequency == 0 else math.sqrt(0.5)
    return factor * math.cos(math.pi * (2 * position + 1) * frequency / 8.0)


def pack_strips(coef_ref, keep_ref, send_ref):
    lane_even = lax.broadcasted_iota(jnp.int32, (8, 128), 1) % 2 == 0
    row_low = lax.broadcasted_iota(jnp.int32, (8, 128), 0) % 4 < 2
    for group in range(16):
        rows = slice(8 * group, 8 * group + 8)
        count = keep_ref[rows, :]
        first = [coef_ref[k, rows, :] for k in range(8)]
        second = [pltpu.roll(value, 127, 1) for value in first]
        packed = [first[0]]
        packed += [jnp.where(count > k, first[k], second[8 - k]) for k in range(1, 8)]
        packed += [second[0], count.astype(jnp.float32)]
        for q in range(5):
            low, high = packed[2 * q], packed[2 * q + 1]
            own = jnp.where(row_low, low, pltpu.roll(high, 2, 0))
            other = jnp.where(row_low, pltpu.roll(low, 6, 0), high)
            merged = jnp.where(lane_even, own, pltpu.roll(other, 1, 1))
            send_ref[2 * group, q] = merged[0:4]
            send_ref[2 * group + 1, q] = merged[4:8]


def unpack_blocks(i, recv_ref, slots_ref):
    row_low = lax.broadcasted_iota(jnp.int32, (8, 128), 0) % 4 < 2
    tiles = [jnp.concatenate([recv_ref[i, q], recv_ref[16 + i, q]], axis=0) for q in range(5)]
    down = [pltpu.roll(value, 2, 0) for value in tiles]
    up = [pltpu.roll(value, 6, 0) for value in tiles]
    count = jnp.where(row_low, up[4], tiles[4])
    kept = jnp.where(row_low, count, 9.0 - count)
    for k in range(8):
        if k % 2 == 0:
            value = jnp.where(row_low, tiles[k // 2], down[(8 - k) // 2])
        else:
            value = jnp.where(row_low, up[k // 2], tiles[(7 - k) // 2])
        if k > 0:
            value = jnp.where(kept > k, value, 0.0)
        slots_ref[i, k] = value


def shade(density, state, sample_count):
    opacity, red, green, blue = state
    u = jnp.exp2(density)
    third = u * (LOG2E - u * (LOG2E / 2 - u * (LOG2E / 3)))
    soft = jnp.where(u < 2.0**-8, third, jnp.log2(1.0 + u))
    t = 1.5 * math.log(2.0) / sample_count
    alpha = soft * (t - soft * (t**2 / 2 - soft * (t**3 / 6 - soft * (t**4 / 24))))
    weight = (1.0 - opacity) * alpha
    v = jnp.exp2(0.5 * density - 1.5 * LOG2E)
    red = red + weight * jnp.exp2(density - soft)
    green = green + weight * jnp.exp2(density * density * (-1.0 / (4 * LOG2E)))
    blue = blue + weight * jnp.exp2(-jnp.log2(1.0 + v))
    return opacity + weight, red, green, blue


def render(x, flip, slots_ref, picture_ref, sample_count):
    unit = 2 * LOG2E
    c0 = cosine(0, 0)
    b1x, b2x = cosine(1, x), cosine(2, x)
    p, q, h = cosine(1, 0), cosine(1, 1), cosine(2, 0)
    turn = (1 - 2 * flip).astype(jnp.float32)

    def step(i, states):
        at = i + flip * (15 - 2 * i)
        a = [slots_ref[at, k] for k in range(8)]
        base = (unit * c0**3) * a[0] + (unit * c0**2 * b1x) * a[2] + (unit * c0**2 * b2x) * a[6]
        along = (unit * c0**2) * a[1] + (unit * c0 * b1x) * a[5]
        curve = (unit * c0**2 * h) * a[4]
        deep, tilt = (unit * c0**2 * turn) * a[3], (unit * c0 * turn) * a[7]
        outer, inner = base + curve, base - curve
        plane = [outer + p * along, inner + q * along, inner - q * along, outer - p * along]
        slope = [deep + p * tilt, deep + q * tilt, deep - q * tilt, deep - p * tilt]
        result = []
        for y in range(4):
            state = states[y]
            far, near = p * slope[y], q * slope[y]
            for density in (plane[y] + far, plane[y] + near, plane[y] - near, plane[y] - far):
                state = shade(density, state, sample_count)
            result.append(state)
        return tuple(result)

    zero = jnp.zeros((8, 128), jnp.float32)
    states = lax.fori_loop(0, 16, step, tuple((zero,) * 4 for _ in range(4)))
    for y in range(4):
        opacity, red, green, blue = states[y]
        clear = 1.0 - opacity
        for channel, value in enumerate((red, green, blue, opacity)):
            joined = value + clear * pltpu.roll(value, 4, 0)
            joined = jnp.where(flip > 0, pltpu.roll(joined, 4, 0), joined)
            start = channel * 64 + x * 16 + y * 4
            picture_ref[start : start + 4, :] = joined[0:4]


def kernel(
    sample_count,
    tiles,
    depths,
    coef_ref,
    keep_ref,
    flip_ref,
    out_ref,
    send_ref,
    recv_ref,
    slots_ref,
    picture_ref,
    send2_ref,
    recv2_ref,
    send_sem,
    recv_sem,
    send2_sem,
    recv2_sem,
):
    tile = lax.axis_index("tile")
    depth = lax.axis_index("depth")

    def tile_at(k):
        return (tile // 8 + k // 8) % 4 * 8 + (tile % 8 + k % 8) % 8

    def tile_from(k):
        return (tile // 8 + 4 - k // 8) % 4 * 8 + (tile % 8 + 8 - k % 8) % 8

    barrier = pltpu.get_barrier_semaphore()

    def greet_tile(k, carry):
        pl.semaphore_signal(
            barrier, inc=1, device_id=(tile_at(k), depth), device_id_type=MESH
        )
        return carry

    def greet_depth(k, carry):
        pl.semaphore_signal(
            barrier, inc=1, device_id=(tile, (depth + k) % depths), device_id_type=MESH
        )
        return carry

    lax.fori_loop(1, tiles, greet_tile, 0)
    lax.fori_loop(1, depths, greet_depth, 0)
    pack_strips(coef_ref, keep_ref, send_ref)
    pl.semaphore_wait(barrier, tiles + depths - 2)

    def strip_copy(to, source):
        return pltpu.make_async_remote_copy(
            src_ref=send_ref.at[to],
            dst_ref=recv_ref.at[source],
            send_sem=send_sem.at[to],
            recv_sem=recv_sem.at[source],
            device_id=(to, depth),
            device_id_type=MESH,
        )

    def strip_start(k, carry):
        strip_copy(tile_at(k), tile).start()
        return carry

    def strip_arrive(k, carry):
        strip_copy(tile_at(k), tile_from(k)).wait_recv()
        return carry

    def strip_sent(k, carry):
        strip_copy(tile_at(k), tile).wait_send()
        return carry

    lax.fori_loop(1, tiles, strip_start, 0)
    recv_ref[tile] = send_ref[tile]
    lax.fori_loop(1, tiles, strip_arrive, 0)

    def unpack_step(i, carry):
        unpack_blocks(i, recv_ref, slots_ref)
        return carry

    lax.fori_loop(0, 16, unpack_step, 0)
    flip = flip_ref[0]
    for x in range(4):
        render(x, flip, slots_ref, picture_ref, sample_count)

    for half in range(2):
        turned = picture_ref[128 * half : 128 * half + 128, :].T
        for band in range(16):
            send2_ref[band, half] = turned[8 * band : 8 * band + 8]

    def band_copy(to, source):
        return pltpu.make_async_remote_copy(
            src_ref=send2_ref.at[to],
            dst_ref=recv2_ref.at[source],
            send_sem=send2_sem.at[to],
            recv_sem=recv2_sem.at[source],
            device_id=(tile, to),
            device_id_type=MESH,
        )

    def band_start(k, carry):
        band_copy((depth + k) % depths, depth).start()
        return carry

    def band_arrive(k, carry):
        band_copy((depth + k) % depths, (depth + depths - k) % depths).wait_recv()
        return carry

    def band_sent(k, carry):
        band_copy((depth + k) % depths, depth).wait_send()
        return carry

    lax.fori_loop(1, depths, band_start, 0)
    recv2_ref[depth] = send2_ref[depth]
    lax.fori_loop(1, tiles, strip_sent, 0)
    lax.fori_loop(1, depths, band_arrive, 0)

    lane_high = lax.broadcasted_iota(jnp.int32, (8, 128), 1) >= 64
    passing = jnp.ones((8, 128), jnp.float32)
    total = [jnp.zeros((8, 128), jnp.float32) for _ in range(2)]
    for brick in range(16):
        at = brick + flip * (15 - 2 * brick)
        front, back = recv2_ref[at, 0], recv2_ref[at, 1]
        opacity = jnp.where(lane_high, back, pltpu.roll(back, 64, 1))
        total = [total[0] + passing * front, total[1] + passing * back]
        passing = passing * (1.0 - opacity)
    out_ref[0] = total[0]
    out_ref[1] = total[1]
    lax.fori_loop(1, depths, band_sent, 0)


def per_device(coefficients, keep_count, view_flip):
    tiles, depths = lax.axis_size("tile"), lax.axis_size("depth")
    sample_count = 4 * tiles * depths
    whole = pl.BlockSpec(memory_space=pltpu.VMEM)
    image = pl.pallas_call(
        functools.partial(kernel, sample_count, tiles, depths),
        out_shape=jax.ShapeDtypeStruct((2, 8, 128), jnp.float32),
        in_specs=[whole, whole, pl.BlockSpec(memory_space=pltpu.SMEM)],
        out_specs=whole,
        scratch_shapes=[
            pltpu.VMEM((32, 5, 4, 128), jnp.float32),
            pltpu.VMEM((32, 5, 4, 128), jnp.float32),
            pltpu.VMEM((16, 8, 8, 128), jnp.float32),
            pltpu.VMEM((256, 128), jnp.float32),
            pltpu.VMEM((16, 2, 8, 128), jnp.float32),
            pltpu.VMEM((16, 2, 8, 128), jnp.float32),
            pltpu.SemaphoreType.DMA((32,)),
            pltpu.SemaphoreType.DMA((32,)),
            pltpu.SemaphoreType.DMA((16,)),
            pltpu.SemaphoreType.DMA((16,)),
        ],
        compiler_params=pltpu.CompilerParams(collective_id=0, has_side_effects=True),
    )(coefficients.reshape(8, 128, 128), keep_count.reshape(128, 128), view_flip)
    parts = image.reshape(2, 4, 2, 2, 4, 4, 2, 2)
    return parts.transpose(0, 3, 2, 7, 4, 1, 6, 5).reshape(4, 16, 32)


def solution(mesh):
    placed = (P(None, "depth", "tile", None, None), P("depth", "tile", None, None), P("tile"))
    return jax.shard_map(
        per_device, mesh=mesh, in_specs=placed, out_specs=P(None, "tile", "depth"), check_vma=False
    )
```

```python
import functools
import math

import jax
import jax.numpy as jnp
from jax import lax
from jax.experimental import pallas as pl
from jax.experimental.pallas import tpu as pltpu
from jax.sharding import PartitionSpec as P

MESH = pl.DeviceIdType.MESH
UNROLL = 4
LOG2E = math.log2(math.e)


def cosine(frequency, position):
    factor = 0.5 if frequency == 0 else math.sqrt(0.5)
    return factor * math.cos(math.pi * (2 * position + 1) * frequency / 8.0)


def pack_strips(coef_ref, keep_ref, send_ref):
    lane_even = lax.broadcasted_iota(jnp.int32, (8, 128), 1) % 2 == 0
    row_low = lax.broadcasted_iota(jnp.int32, (8, 128), 0) % 4 < 2
    for group in range(16):
        rows = slice(8 * group, 8 * group + 8)
        count = keep_ref[rows, :]
        first = [coef_ref[k, rows, :] for k in range(8)]
        second = [pltpu.roll(value, 127, 1) for value in first]
        packed = [first[0]]
        packed += [jnp.where(count > k, first[k], second[8 - k]) for k in range(1, 8)]
        packed += [second[0], count.astype(jnp.float32)]
        for q in range(5):
            low, high = packed[2 * q], packed[2 * q + 1]
            own = jnp.where(row_low, low, pltpu.roll(high, 2, 0))
            other = jnp.where(row_low, pltpu.roll(low, 6, 0), high)
            merged = jnp.where(lane_even, own, pltpu.roll(other, 1, 1))
            send_ref[2 * group, q] = merged[0:4]
            send_ref[2 * group + 1, q] = merged[4:8]


def unpack_blocks(i, recv_ref, slots_ref):
    row_low = lax.broadcasted_iota(jnp.int32, (8, 128), 0) % 4 < 2
    tiles = [jnp.concatenate([recv_ref[i, q], recv_ref[16 + i, q]], axis=0) for q in range(5)]
    down = [pltpu.roll(value, 2, 0) for value in tiles]
    up = [pltpu.roll(value, 6, 0) for value in tiles]
    count = jnp.where(row_low, up[4], tiles[4])
    kept = jnp.where(row_low, count, 9.0 - count)
    for k in range(8):
        if k % 2 == 0:
            value = jnp.where(row_low, tiles[k // 2], down[(8 - k) // 2])
        else:
            value = jnp.where(row_low, up[k // 2], tiles[(7 - k) // 2])
        if k > 0:
            value = jnp.where(kept > k, value, 0.0)
        slots_ref[i, k] = value


def shade(density, state, sample_count):
    opacity, red, green, blue = state
    u = jnp.exp2(density)
    third = u * (LOG2E - u * (LOG2E / 2 - u * (LOG2E / 3)))
    soft = jnp.where(u < 2.0**-8, third, jnp.log2(1.0 + u))
    t = 1.5 * math.log(2.0) / sample_count
    alpha = soft * (t - soft * (t**2 / 2 - soft * (t**3 / 6 - soft * (t**4 / 24))))
    weight = (1.0 - opacity) * alpha
    v = jnp.exp2(0.5 * density - 1.5 * LOG2E)
    red = red + weight * jnp.exp2(density - soft)
    green = green + weight * jnp.exp2(density * density * (-1.0 / (4 * LOG2E)))
    blue = blue + weight * jnp.exp2(-jnp.log2(1.0 + v))
    return opacity + weight, red, green, blue


def render(x, flip, slots_ref, picture_ref, sample_count):
    unit = 2 * LOG2E
    c0 = cosine(0, 0)
    b1x, b2x = cosine(1, x), cosine(2, x)
    p, q, h = cosine(1, 0), cosine(1, 1), cosine(2, 0)
    turn = (1 - 2 * flip).astype(jnp.float32)

    def step(i, states):
        at = i + flip * (15 - 2 * i)
        a = [slots_ref[at, k] for k in range(8)]
        base = (unit * c0**3) * a[0] + (unit * c0**2 * b1x) * a[2] + (unit * c0**2 * b2x) * a[6]
        along = (unit * c0**2) * a[1] + (unit * c0 * b1x) * a[5]
        curve = (unit * c0**2 * h) * a[4]
        deep, tilt = (unit * c0**2 * turn) * a[3], (unit * c0 * turn) * a[7]
        outer, inner = base + curve, base - curve
        plane = [outer + p * along, inner + q * along, inner - q * along, outer - p * along]
        slope = [deep + p * tilt, deep + q * tilt, deep - q * tilt, deep - p * tilt]
        result = []
        for y in range(4):
            state = states[y]
            far, near = p * slope[y], q * slope[y]
            for density in (plane[y] + far, plane[y] + near, plane[y] - near, plane[y] - far):
                state = shade(density, state, sample_count)
            result.append(state)
        return tuple(result)

    zero = jnp.zeros((8, 128), jnp.float32)
    states = lax.fori_loop(0, 16, step, tuple((zero,) * 4 for _ in range(4)), unroll=UNROLL)
    for y in range(4):
        opacity, red, green, blue = states[y]
        clear = 1.0 - opacity
        for channel, value in enumerate((red, green, blue, opacity)):
            joined = value + clear * pltpu.roll(value, 4, 0)
            joined = jnp.where(flip > 0, pltpu.roll(joined, 4, 0), joined)
            start = channel * 64 + x * 16 + y * 4
            picture_ref[start : start + 4, :] = joined[0:4]


def kernel(
    sample_count,
    tiles,
    depths,
    coef_ref,
    keep_ref,
    flip_ref,
    out_ref,
    send_ref,
    recv_ref,
    slots_ref,
    picture_ref,
    ordered_ref,
    send2_ref,
    recv2_ref,
    send_sem,
    recv_sem,
    send2_sem,
    recv2_sem,
):
    tile = lax.axis_index("tile")
    depth = lax.axis_index("depth")

    xs = [lax.rem(lax.div(tile, 8) + k, 4) * 8 for k in range(4)]
    ys = [lax.rem(lax.rem(tile, 8) + k, 8) for k in range(8)]
    steps = [(dx, dy) for dx in range(4) for dy in range(8)][1:]
    steps.sort(key=lambda step: -min(step[0], 4 - step[0]) - min(step[1], 8 - step[1]))
    peers = [xs[dx] + ys[dy] for dx, dy in steps]
    bands = [lax.rem(depth + k, depths) for k in (8, 7, 9, 6, 10, 5, 11, 4, 12, 3, 13, 2, 14, 1, 15)]

    barrier = pltpu.get_barrier_semaphore()
    for to in peers:
        pl.semaphore_signal(barrier, inc=1, device_id=(to, depth), device_id_type=MESH)
    for to in bands:
        pl.semaphore_signal(barrier, inc=1, device_id=(tile, to), device_id_type=MESH)
    pack_strips(coef_ref, keep_ref, send_ref)
    pl.semaphore_wait(barrier, tiles + depths - 2)

    def strip_copy(to, source):
        return pltpu.make_async_remote_copy(
            src_ref=send_ref.at[to],
            dst_ref=recv_ref.at[source],
            send_sem=send_sem.at[to],
            recv_sem=recv_sem.at[source],
            device_id=(to, depth),
            device_id_type=MESH,
        )

    for to in peers:
        strip_copy(to, tile).start()
    recv_ref[tile] = send_ref[tile]
    for source in peers:
        strip_copy(source, source).wait_recv()

    def unpack_step(i, carry):
        unpack_blocks(i, recv_ref, slots_ref)
        return carry

    lax.fori_loop(0, 16, unpack_step, 0)
    flip = flip_ref[0]
    for x in range(4):
        render(x, flip, slots_ref, picture_ref, sample_count)

    for channel in range(4):
        for x in range(4):
            for column in range(2):
                for block in range(2):
                    source = channel * 64 + x * 16 + block * 2 + column
                    start = channel * 64 + (7 - column * 4 - x) * 8 + block * 4
                    ordered_ref[start : start + 4, :] = picture_ref[pl.ds(source, 4, stride=4), :]

    for half in range(2):
        turned = ordered_ref[128 * half : 128 * half + 128, :].T
        for band in range(16):
            send2_ref[band, half] = turned[8 * band : 8 * band + 8]

    def band_copy(to, source):
        return pltpu.make_async_remote_copy(
            src_ref=send2_ref.at[to],
            dst_ref=recv2_ref.at[source],
            send_sem=send2_sem.at[to],
            recv_sem=recv2_sem.at[source],
            device_id=(tile, to),
            device_id_type=MESH,
        )

    for to in bands:
        band_copy(to, depth).start()
    recv2_ref[depth] = send2_ref[depth]
    for to in peers:
        strip_copy(to, tile).wait_send()
    for source in bands:
        band_copy(source, source).wait_recv()

    lane_high = lax.broadcasted_iota(jnp.int32, (8, 128), 1) >= 64
    passing = jnp.ones((8, 128), jnp.float32)
    total = [jnp.zeros((8, 128), jnp.float32) for _ in range(2)]
    for brick in range(16):
        at = brick + flip * (15 - 2 * brick)
        front, back = recv2_ref[at, 0], recv2_ref[at, 1]
        opacity = jnp.where(lane_high, back, pltpu.roll(back, 64, 1))
        total = [total[0] + passing * front, total[1] + passing * back]
        passing = passing * (1.0 - opacity)
    lane_pair = lax.broadcasted_iota(jnp.int32, (8, 128), 1) // 8
    for channel in range(4):
        values = [jnp.zeros((8, 128), jnp.float32)] * 2
        for pair in range(4):
            shift = (8 * pair - 64 * (channel % 2) - 56) % 128
            moved = pltpu.roll(total[channel // 2], shift, 1)
            for half in range(2):
                row = jnp.broadcast_to(moved[2 * pair + half : 2 * pair + half + 1], (8, 128))
                spread = pltpu.roll(row, 0, 1, stride=8, stride_axis=0)
                values[half] = jnp.where(lane_pair == pair, spread, values[half])
        for half in range(2):
            out_ref[channel, 8 * half : 8 * half + 8, :] = values[half][:, :32]
    for to in bands:
        band_copy(to, depth).wait_send()


def per_device(coefficients, keep_count, view_flip):
    tiles, depths = lax.axis_size("tile"), lax.axis_size("depth")
    sample_count = 4 * tiles * depths
    whole = pl.BlockSpec(memory_space=pltpu.VMEM)
    return pl.pallas_call(
        functools.partial(kernel, sample_count, tiles, depths),
        out_shape=jax.ShapeDtypeStruct((4, 16, 32), jnp.float32),
        in_specs=[whole, whole, pl.BlockSpec(memory_space=pltpu.SMEM)],
        out_specs=whole,
        scratch_shapes=[
            pltpu.VMEM((32, 5, 4, 128), jnp.float32),
            pltpu.VMEM((32, 5, 4, 128), jnp.float32),
            pltpu.VMEM((16, 8, 8, 128), jnp.float32),
            pltpu.VMEM((256, 128), jnp.float32),
            pltpu.VMEM((256, 128), jnp.float32),
            pltpu.VMEM((16, 2, 8, 128), jnp.float32),
            pltpu.VMEM((16, 2, 8, 128), jnp.float32),
            pltpu.SemaphoreType.DMA((32,)),
            pltpu.SemaphoreType.DMA((32,)),
            pltpu.SemaphoreType.DMA((16,)),
            pltpu.SemaphoreType.DMA((16,)),
        ],
        compiler_params=pltpu.CompilerParams(collective_id=0, has_side_effects=True),
    )(coefficients.reshape(8, 128, 128), keep_count.reshape(128, 128), view_flip)


def solution(mesh):
    placed = (P(None, "depth", "tile", None, None), P("depth", "tile", None, None), P("tile"))
    return jax.shard_map(
        per_device, mesh=mesh, in_specs=placed, out_specs=P(None, "tile", "depth"), check_vma=False
    )
```

```python
import functools
import math

import jax
import jax.numpy as jnp
from jax import lax
from jax.experimental import pallas as pl
from jax.experimental.pallas import tpu as pltpu
from jax.sharding import PartitionSpec as P

MESH = pl.DeviceIdType.MESH
UNROLL = 4
LOG2E = math.log2(math.e)


def cosine(frequency, position):
    factor = 0.5 if frequency == 0 else math.sqrt(0.5)
    return factor * math.cos(math.pi * (2 * position + 1) * frequency / 8.0)


def pack_strips(coef_ref, keep_ref, send_ref):
    lane_even = lax.broadcasted_iota(jnp.int32, (8, 128), 1) % 2 == 0
    row_low = lax.broadcasted_iota(jnp.int32, (8, 128), 0) % 2 == 0
    for group in range(16):
        rows = slice(8 * group, 8 * group + 8)
        count = keep_ref[rows, :]
        first = [coef_ref[k, rows, :] for k in range(8)]
        second = [pltpu.roll(value, 127, 1) for value in first]
        packed = [first[0]]
        packed += [jnp.where(count > k, first[k], second[8 - k]) for k in range(1, 8)]
        packed += [second[0], count.astype(jnp.float32)]
        for q in range(5):
            low, high = packed[2 * q], packed[2 * q + 1]
            own = jnp.where(row_low, low, pltpu.roll(high, 1, 0))
            other = jnp.where(row_low, pltpu.roll(low, 7, 0), high)
            merged = jnp.where(lane_even, own, pltpu.roll(other, 1, 1))
            for part in range(4):
                send_ref[part % 2, 2 * group + part // 2, q] = merged[2 * part : 2 * part + 2]


def unpack_blocks(half, i, recv_ref, slots_ref):
    row_low = lax.broadcasted_iota(jnp.int32, (8, 128), 0) % 2 == 0
    tiles = [
        jnp.concatenate([recv_ref[half, 8 * segment + i, q] for segment in range(4)], axis=0)
        for q in range(5)
    ]
    down = [pltpu.roll(value, 1, 0) for value in tiles]
    up = [pltpu.roll(value, 7, 0) for value in tiles]
    count = jnp.where(row_low, up[4], tiles[4])
    kept = jnp.where(row_low, count, 9.0 - count)
    for k in range(8):
        if k % 2 == 0:
            value = jnp.where(row_low, tiles[k // 2], down[(8 - k) // 2])
        else:
            value = jnp.where(row_low, up[k // 2], tiles[(7 - k) // 2])
        if k > 0:
            value = jnp.where(kept > k, value, 0.0)
        slots_ref[i, k] = value


def shade(density, state, sample_count):
    opacity, red, green, blue = state
    u = jnp.exp2(density)
    third = u * (LOG2E - u * (LOG2E / 2 - u * (LOG2E / 3)))
    soft = jnp.where(u < 2.0**-8, third, jnp.log2(1.0 + u))
    t = 1.5 * math.log(2.0) / sample_count
    alpha = soft * (t - soft * (t**2 / 2 - soft * (t**3 / 6 - soft * (t**4 / 24))))
    weight = (1.0 - opacity) * alpha
    v = jnp.exp2(0.5 * density - 1.5 * LOG2E)
    red = red + weight * jnp.exp2(density - soft)
    green = green + weight * jnp.exp2(density * density * (-1.0 / (4 * LOG2E)))
    blue = blue + weight * jnp.exp2(-jnp.log2(1.0 + v))
    return opacity + weight, red, green, blue


def render(x, flip, slots_ref, picture_ref, sample_count):
    unit = 2 * LOG2E
    c0 = cosine(0, 0)
    b1x, b2x = cosine(1, x), cosine(2, x)
    p, q, h = cosine(1, 0), cosine(1, 1), cosine(2, 0)
    turn = (1 - 2 * flip).astype(jnp.float32)

    def step(i, states):
        at = i + flip * (7 - 2 * i)
        a = [slots_ref[at, k] for k in range(8)]
        base = (unit * c0**3) * a[0] + (unit * c0**2 * b1x) * a[2] + (unit * c0**2 * b2x) * a[6]
        along = (unit * c0**2) * a[1] + (unit * c0 * b1x) * a[5]
        curve = (unit * c0**2 * h) * a[4]
        deep, tilt = (unit * c0**2 * turn) * a[3], (unit * c0 * turn) * a[7]
        outer, inner = base + curve, base - curve
        plane = [outer + p * along, inner + q * along, inner - q * along, outer - p * along]
        slope = [deep + p * tilt, deep + q * tilt, deep - q * tilt, deep - p * tilt]
        result = []
        for y in range(4):
            state = states[y]
            far, near = p * slope[y], q * slope[y]
            for density in (plane[y] + far, plane[y] + near, plane[y] - near, plane[y] - far):
                state = shade(density, state, sample_count)
            result.append(state)
        return tuple(result)

    zero = jnp.zeros((8, 128), jnp.float32)
    states = lax.fori_loop(0, 8, step, tuple((zero,) * 4 for _ in range(4)), unroll=UNROLL)
    for y in range(4):
        opacity, red, green, blue = states[y]
        values = [red, green, blue, opacity]
        for distance in (2, 4):
            clear = 1.0 - values[3]
            if distance == 2:
                beyond = [
                    jnp.where(flip > 0, pltpu.roll(value, 2, 0), pltpu.roll(value, 6, 0))
                    for value in values
                ]
            else:
                beyond = [pltpu.roll(value, 4, 0) for value in values]
            values = [value + clear * more for value, more in zip(values, beyond)]
        for channel, value in enumerate(values):
            value = jnp.where(flip > 0, pltpu.roll(value, 2, 0), value)
            start = channel * 32 + x * 8 + y * 2
            picture_ref[start : start + 2, :] = value[0:2]


def kernel(
    sample_count,
    tiles,
    depths,
    coef_ref,
    keep_ref,
    flip_ref,
    out_ref,
    send_ref,
    recv_ref,
    slots_ref,
    picture_ref,
    ordered_ref,
    send2_ref,
    recv2_first,
    recv2_second,
    send_sem,
    recv_sem,
    send2_sem,
    recv2_sem,
):
    tile = lax.axis_index("tile")
    depth = lax.axis_index("depth")
    recv2 = (recv2_first, recv2_second)

    xs = [lax.rem(lax.div(tile, 8) + k, 4) * 8 for k in range(4)]
    ys = [lax.rem(lax.rem(tile, 8) + k, 8) for k in range(8)]
    steps = [(dx, dy) for dx in range(4) for dy in range(8)][1:]
    steps.sort(key=lambda step: -min(step[0], 4 - step[0]) - min(step[1], 8 - step[1]))
    peers = [xs[dx] + ys[dy] for dx, dy in steps]
    bands = [lax.rem(depth + k, depths) for k in (8, 7, 9, 6, 10, 5, 11, 4, 12, 3, 13, 2, 14, 1, 15)]

    barrier = pltpu.get_barrier_semaphore()
    for to in peers:
        pl.semaphore_signal(barrier, inc=1, device_id=(to, depth), device_id_type=MESH)
    for to in bands:
        pl.semaphore_signal(barrier, inc=1, device_id=(tile, to), device_id_type=MESH)
    pack_strips(coef_ref, keep_ref, send_ref)
    pl.semaphore_wait(barrier, tiles + depths - 2)

    def strip_copy(half, to, source):
        return pltpu.make_async_remote_copy(
            src_ref=send_ref.at[half, to],
            dst_ref=recv_ref.at[half, source],
            send_sem=send_sem.at[half, to],
            recv_sem=recv_sem.at[half, source],
            device_id=(to, depth),
            device_id_type=MESH,
        )

    def band_copy(half, to, source):
        return pltpu.make_async_remote_copy(
            src_ref=send2_ref.at[half, to],
            dst_ref=recv2[half].at[source],
            send_sem=send2_sem.at[half, to],
            recv_sem=recv2_sem.at[half, source],
            device_id=(tile, to),
            device_id_type=MESH,
        )

    for half in range(2):
        for to in peers:
            strip_copy(half, to, tile).start()
        recv_ref[half, tile] = send_ref[half, tile]

    flip = flip_ref[0]
    for half in range(2):
        for source in peers:
            strip_copy(half, source, source).wait_recv()

        def unpack_step(i, carry):
            unpack_blocks(half, i, recv_ref, slots_ref)
            return carry

        lax.fori_loop(0, 8, unpack_step, 0)
        for x in range(4):
            render(x, flip, slots_ref, picture_ref, sample_count)
        for channel in range(4):
            for x in range(4):
                for block in range(2):
                    source = channel * 32 + x * 8 + block
                    start = channel * 32 + (3 - x) * 8 + block * 4
                    ordered_ref[start : start + 4, :] = picture_ref[pl.ds(source, 4, stride=2), :]
        turned = ordered_ref[...].T
        for band in range(16):
            send2_ref[half, band] = turned[8 * band : 8 * band + 8]
        for to in bands:
            band_copy(half, to, depth).start()
        recv2[half][depth] = send2_ref[half, depth]

    for half in range(2):
        for to in peers:
            strip_copy(half, to, tile).wait_send()
    lane = lax.broadcasted_iota(jnp.int32, (8, 128), 1)
    row_first = lax.broadcasted_iota(jnp.int32, (8, 128), 0) < 4
    for half in range(2):
        for source in bands:
            band_copy(half, source, source).wait_recv()
        passing = jnp.ones((8, 128), jnp.float32)
        total = jnp.zeros((8, 128), jnp.float32)
        for brick in range(16):
            front = recv2[half][brick + flip * (15 - 2 * brick)]
            opacity = jnp.where(lane >= 96, front, pltpu.roll(front, 64, 1))
            opacity = jnp.where(lane // 32 % 2 == 1, opacity, pltpu.roll(opacity, 32, 1))
            total = total + passing * front
            passing = passing * (1.0 - opacity)
        for channel in range(4):
            value = jnp.zeros((8, 128), jnp.float32)
            for pair in range(4):
                shift = 8 * pair - 32 * channel - 24
                first = pltpu.roll(total, shift % 128, 1)[2 * pair : 2 * pair + 1]
                second = pltpu.roll(total, (shift - 32) % 128, 1)[2 * pair + 1 : 2 * pair + 2]
                rows = jnp.where(
                    row_first, jnp.broadcast_to(first, (8, 128)), jnp.broadcast_to(second, (8, 128))
                )
                spread = pltpu.roll(rows, 0, 1, stride=8, stride_axis=0)
                value = jnp.where(lane // 8 == pair, spread, value)
            out_ref[channel, 8 * half : 8 * half + 8, :] = value[:, :32]
    for half in range(2):
        for to in bands:
            band_copy(half, to, depth).wait_send()


def per_device(coefficients, keep_count, view_flip):
    tiles, depths = lax.axis_size("tile"), lax.axis_size("depth")
    sample_count = 4 * tiles * depths
    whole = pl.BlockSpec(memory_space=pltpu.VMEM)
    return pl.pallas_call(
        functools.partial(kernel, sample_count, tiles, depths),
        out_shape=jax.ShapeDtypeStruct((4, 16, 32), jnp.float32),
        in_specs=[whole, whole, pl.BlockSpec(memory_space=pltpu.SMEM)],
        out_specs=whole,
        scratch_shapes=[
            pltpu.VMEM((2, 32, 5, 2, 128), jnp.float32),
            pltpu.VMEM((2, 32, 5, 2, 128), jnp.float32),
            pltpu.VMEM((8, 8, 8, 128), jnp.float32),
            pltpu.VMEM((128, 128), jnp.float32),
            pltpu.VMEM((128, 128), jnp.float32),
            pltpu.VMEM((2, 16, 8, 128), jnp.float32),
            pltpu.VMEM((16, 8, 128), jnp.float32),
            pltpu.VMEM((16, 8, 128), jnp.float32),
            pltpu.SemaphoreType.DMA((2, 32)),
            pltpu.SemaphoreType.DMA((2, 32)),
            pltpu.SemaphoreType.DMA((2, 16)),
            pltpu.SemaphoreType.DMA((2, 16)),
        ],
        compiler_params=pltpu.CompilerParams(collective_id=0, has_side_effects=True),
    )(coefficients.reshape(8, 128, 128), keep_count.reshape(128, 128), view_flip)


def solution(mesh):
    placed = (P(None, "depth", "tile", None, None), P("depth", "tile", None, None), P("tile"))
    return jax.shard_map(
        per_device, mesh=mesh, in_specs=placed, out_specs=P(None, "tile", "depth"), check_vma=False
    )
```

```python
import functools
import math

import jax
import jax.numpy as jnp
from jax import lax
from jax.experimental import pallas as pl
from jax.experimental.pallas import tpu as pltpu
from jax.sharding import PartitionSpec as P

MESH = pl.DeviceIdType.MESH
UNROLL = 4
LOG2E = math.log2(math.e)


def cosine(frequency, position):
    factor = 0.5 if frequency == 0 else math.sqrt(0.5)
    return factor * math.cos(math.pi * (2 * position + 1) * frequency / 8.0)


def pack_strips(coef_ref, keep_ref, send_ref):
    lane_even = lax.broadcasted_iota(jnp.int32, (8, 128), 1) % 2 == 0
    row_low = lax.broadcasted_iota(jnp.int32, (8, 128), 0) % 2 == 0
    for group in range(16):
        rows = slice(8 * group, 8 * group + 8)
        count = keep_ref[rows, :]
        first = [coef_ref[k, rows, :] for k in range(8)]
        second = [pltpu.roll(value, 127, 1) for value in first]
        packed = [first[0]]
        packed += [jnp.where(count > k, first[k], second[8 - k]) for k in range(1, 8)]
        packed += [second[0], count.astype(jnp.float32)]
        for q in range(5):
            low, high = packed[2 * q], packed[2 * q + 1]
            own = jnp.where(row_low, low, pltpu.roll(high, 1, 0))
            other = jnp.where(row_low, pltpu.roll(low, 7, 0), high)
            merged = jnp.where(lane_even, own, pltpu.roll(other, 1, 1))
            for part in range(4):
                send_ref[part % 2, 2 * group + part // 2, q] = merged[2 * part : 2 * part + 2]


def unpack_blocks(half, i, recv_ref, slots_ref):
    row_low = lax.broadcasted_iota(jnp.int32, (8, 128), 0) % 2 == 0
    tiles = [
        jnp.concatenate([recv_ref[half, 8 * segment + i, q] for segment in range(4)], axis=0)
        for q in range(5)
    ]
    down = [pltpu.roll(value, 1, 0) for value in tiles]
    up = [pltpu.roll(value, 7, 0) for value in tiles]
    count = jnp.where(row_low, up[4], tiles[4])
    kept = jnp.where(row_low, count, 9.0 - count)
    for k in range(8):
        if k % 2 == 0:
            value = jnp.where(row_low, tiles[k // 2], down[(8 - k) // 2])
        else:
            value = jnp.where(row_low, up[k // 2], tiles[(7 - k) // 2])
        if k > 0:
            value = jnp.where(kept > k, value, 0.0)
        slots_ref[i, k] = value


def shade(density, state, sample_count):
    opacity, red, green, blue = state
    u = jnp.exp2(density)
    third = u * (LOG2E - u * (LOG2E / 2 - u * (LOG2E / 3)))
    soft = jnp.where(u < 2.0**-8, third, jnp.log2(1.0 + u))
    t = 1.5 * math.log(2.0) / sample_count
    alpha = soft * (t - soft * (t**2 / 2 - soft * (t**3 / 6 - soft * (t**4 / 24))))
    weight = (1.0 - opacity) * alpha
    v = jnp.exp2(0.5 * density - 1.5 * LOG2E)
    red = red + weight * jnp.exp2(density - soft)
    green = green + weight * jnp.exp2(density * density * (-1.0 / (4 * LOG2E)))
    blue = blue + weight * jnp.exp2(-jnp.log2(1.0 + v))
    return opacity + weight, red, green, blue


def render(x, flip, slots_ref, picture_ref, sample_count):
    unit = 2 * LOG2E
    c0 = cosine(0, 0)
    b1x, b2x = cosine(1, x), cosine(2, x)
    p, q, h = cosine(1, 0), cosine(1, 1), cosine(2, 0)
    turn = (1 - 2 * flip).astype(jnp.float32)

    def step(i, states):
        at = i + flip * (7 - 2 * i)
        a = [slots_ref[at, k] for k in range(8)]
        base = (unit * c0**3) * a[0] + (unit * c0**2 * b1x) * a[2] + (unit * c0**2 * b2x) * a[6]
        along = (unit * c0**2) * a[1] + (unit * c0 * b1x) * a[5]
        curve = (unit * c0**2 * h) * a[4]
        deep, tilt = (unit * c0**2 * turn) * a[3], (unit * c0 * turn) * a[7]
        outer, inner = base + curve, base - curve
        plane = [outer + p * along, inner + q * along, inner - q * along, outer - p * along]
        slope = [deep + p * tilt, deep + q * tilt, deep - q * tilt, deep - p * tilt]
        result = []
        for y in range(4):
            state = states[y]
            far, near = p * slope[y], q * slope[y]
            for density in (plane[y] + far, plane[y] + near, plane[y] - near, plane[y] - far):
                state = shade(density, state, sample_count)
            result.append(state)
        return tuple(result)

    zero = jnp.zeros((8, 128), jnp.float32)
    states = lax.fori_loop(0, 8, step, tuple((zero,) * 4 for _ in range(4)), unroll=UNROLL)
    for y in range(4):
        opacity, red, green, blue = states[y]
        values = [red, green, blue, opacity]
        for distance in (2, 4):
            clear = 1.0 - values[3]
            if distance == 2:
                beyond = [
                    jnp.where(flip > 0, pltpu.roll(value, 2, 0), pltpu.roll(value, 6, 0))
                    for value in values
                ]
            else:
                beyond = [pltpu.roll(value, 4, 0) for value in values]
            values = [value + clear * more for value, more in zip(values, beyond)]
        for channel, value in enumerate(values):
            value = jnp.where(flip > 0, pltpu.roll(value, 2, 0), value)
            start = channel * 32 + x * 8 + y * 2
            picture_ref[start : start + 2, :] = value[0:2]


def kernel(
    sample_count,
    tiles,
    depths,
    coef_hbm,
    keep_hbm,
    flip_ref,
    out_ref,
    coef_ref,
    keep_ref,
    coef_sem,
    keep_sem,
    send_ref,
    recv_ref,
    slots_ref,
    picture_ref,
    ordered_ref,
    send2_ref,
    recv2_first,
    recv2_second,
    send_sem,
    recv_sem,
    send2_sem,
    recv2_sem,
):
    loads = [
        pltpu.make_async_copy(coef_hbm, coef_ref, coef_sem),
        pltpu.make_async_copy(keep_hbm, keep_ref, keep_sem),
    ]
    for load in loads:
        load.start()
    tile = lax.axis_index("tile")
    depth = lax.axis_index("depth")
    recv2 = (recv2_first, recv2_second)

    xs = [lax.rem(lax.div(tile, 8) + k, 4) * 8 for k in range(4)]
    ys = [lax.rem(lax.rem(tile, 8) + k, 8) for k in range(8)]
    steps = [(dx, dy) for dx in range(4) for dy in range(8)][1:]
    steps.sort(key=lambda step: -min(step[0], 4 - step[0]) - min(step[1], 8 - step[1]))
    peers = [xs[dx] + ys[dy] for dx, dy in steps]
    bands = [lax.rem(depth + k, depths) for k in (8, 7, 9, 6, 10, 5, 11, 4, 12, 3, 13, 2, 14, 1, 15)]

    barrier = pltpu.get_barrier_semaphore()
    for to in peers:
        pl.semaphore_signal(barrier, inc=1, device_id=(to, depth), device_id_type=MESH)
    for to in bands:
        pl.semaphore_signal(barrier, inc=1, device_id=(tile, to), device_id_type=MESH)
    for load in loads:
        load.wait()
    pack_strips(coef_ref, keep_ref, send_ref)
    pl.semaphore_wait(barrier, tiles + depths - 2)

    def strip_copy(half, to, source):
        return pltpu.make_async_remote_copy(
            src_ref=send_ref.at[half, to],
            dst_ref=recv_ref.at[half, source],
            send_sem=send_sem.at[half, to],
            recv_sem=recv_sem.at[half, source],
            device_id=(to, depth),
            device_id_type=MESH,
        )

    def band_copy(half, to, source):
        return pltpu.make_async_remote_copy(
            src_ref=send2_ref.at[half, to],
            dst_ref=recv2[half].at[source],
            send_sem=send2_sem.at[half, to],
            recv_sem=recv2_sem.at[half, source],
            device_id=(tile, to),
            device_id_type=MESH,
        )

    for half in range(2):
        for to in peers:
            strip_copy(half, to, tile).start()
        recv_ref[half, tile] = send_ref[half, tile]

    flip = flip_ref[0]
    for half in range(2):
        for source in peers:
            strip_copy(half, source, source).wait_recv()

        def unpack_step(i, carry):
            unpack_blocks(half, i, recv_ref, slots_ref)
            return carry

        lax.fori_loop(0, 8, unpack_step, 0)
        for x in range(4):
            render(x, flip, slots_ref, picture_ref, sample_count)
        for channel in range(4):
            for x in range(4):
                for block in range(2):
                    source = channel * 32 + x * 8 + block
                    start = channel * 32 + (3 - x) * 8 + block * 4
                    ordered_ref[start : start + 4, :] = picture_ref[pl.ds(source, 4, stride=2), :]
        turned = ordered_ref[...].T
        for band in range(16):
            send2_ref[half, band] = turned[8 * band : 8 * band + 8]
        for to in bands:
            band_copy(half, to, depth).start()
        recv2[half][depth] = send2_ref[half, depth]

    for half in range(2):
        for to in peers:
            strip_copy(half, to, tile).wait_send()
    lane = lax.broadcasted_iota(jnp.int32, (8, 128), 1)
    row_first = lax.broadcasted_iota(jnp.int32, (8, 128), 0) < 4
    for half in range(2):
        for source in bands:
            band_copy(half, source, source).wait_recv()
        passing = jnp.ones((8, 128), jnp.float32)
        total = jnp.zeros((8, 128), jnp.float32)
        for brick in range(16):
            front = recv2[half][brick + flip * (15 - 2 * brick)]
            opacity = jnp.where(lane >= 96, front, pltpu.roll(front, 64, 1))
            opacity = jnp.where(lane // 32 % 2 == 1, opacity, pltpu.roll(opacity, 32, 1))
            total = total + passing * front
            passing = passing * (1.0 - opacity)
        for channel in range(4):
            value = jnp.zeros((8, 128), jnp.float32)
            for pair in range(4):
                shift = 8 * pair - 32 * channel - 24
                first = pltpu.roll(total, shift % 128, 1)[2 * pair : 2 * pair + 1]
                second = pltpu.roll(total, (shift - 32) % 128, 1)[2 * pair + 1 : 2 * pair + 2]
                rows = jnp.where(
                    row_first, jnp.broadcast_to(first, (8, 128)), jnp.broadcast_to(second, (8, 128))
                )
                spread = pltpu.roll(rows, 0, 1, stride=8, stride_axis=0)
                value = jnp.where(lane // 8 == pair, spread, value)
            out_ref[channel, 8 * half : 8 * half + 8, :] = value[:, :32]
    for half in range(2):
        for to in bands:
            band_copy(half, to, depth).wait_send()


def per_device(coefficients, keep_count, view_flip):
    tiles, depths = lax.axis_size("tile"), lax.axis_size("depth")
    sample_count = 4 * tiles * depths
    whole = pl.BlockSpec(memory_space=pltpu.VMEM)
    far = pl.BlockSpec(memory_space=pltpu.HBM)
    return pl.pallas_call(
        functools.partial(kernel, sample_count, tiles, depths),
        out_shape=jax.ShapeDtypeStruct((4, 16, 32), jnp.float32),
        in_specs=[far, far, pl.BlockSpec(memory_space=pltpu.SMEM)],
        out_specs=whole,
        scratch_shapes=[
            pltpu.VMEM((8, 128, 128), jnp.float32),
            pltpu.VMEM((128, 128), jnp.int32),
            pltpu.SemaphoreType.DMA,
            pltpu.SemaphoreType.DMA,
            pltpu.VMEM((2, 32, 5, 2, 128), jnp.float32),
            pltpu.VMEM((2, 32, 5, 2, 128), jnp.float32),
            pltpu.VMEM((8, 8, 8, 128), jnp.float32),
            pltpu.VMEM((128, 128), jnp.float32),
            pltpu.VMEM((128, 128), jnp.float32),
            pltpu.VMEM((2, 16, 8, 128), jnp.float32),
            pltpu.VMEM((16, 8, 128), jnp.float32),
            pltpu.VMEM((16, 8, 128), jnp.float32),
            pltpu.SemaphoreType.DMA((2, 32)),
            pltpu.SemaphoreType.DMA((2, 32)),
            pltpu.SemaphoreType.DMA((2, 16)),
            pltpu.SemaphoreType.DMA((2, 16)),
        ],
        compiler_params=pltpu.CompilerParams(collective_id=0, has_side_effects=True),
    )(coefficients.reshape(8, 128, 128), keep_count.reshape(128, 128), view_flip)


def solution(mesh):
    placed = (P(None, "depth", "tile", None, None), P("depth", "tile", None, None), P("tile"))
    return jax.shard_map(
        per_device, mesh=mesh, in_specs=placed, out_specs=P(None, "tile", "depth"), check_vma=False
    )
```

```python
import functools
import math

import jax
import jax.numpy as jnp
from jax import lax
from jax.experimental import pallas as pl
from jax.experimental.pallas import tpu as pltpu
from jax.sharding import PartitionSpec as P

MESH = pl.DeviceIdType.MESH
UNROLL = 8
LOG2E = math.log2(math.e)


def cosine(frequency, position):
    factor = 0.5 if frequency == 0 else math.sqrt(0.5)
    return factor * math.cos(math.pi * (2 * position + 1) * frequency / 8.0)


def pack_strips(coef_ref, keep_ref, send_ref):
    lane_even = lax.broadcasted_iota(jnp.int32, (8, 128), 1) % 2 == 0
    row_low = lax.broadcasted_iota(jnp.int32, (8, 128), 0) % 2 == 0
    for group in range(16):
        rows = slice(8 * group, 8 * group + 8)
        count = keep_ref[rows, :]
        first = [coef_ref[k, rows, :] for k in range(8)]
        second = [pltpu.roll(value, 127, 1) for value in first]
        packed = [first[0]]
        packed += [jnp.where(count > k, first[k], second[8 - k]) for k in range(1, 8)]
        packed += [second[0], count.astype(jnp.float32)]
        for q in range(5):
            low, high = packed[2 * q], packed[2 * q + 1]
            own = jnp.where(row_low, low, pltpu.roll(high, 1, 0))
            other = jnp.where(row_low, pltpu.roll(low, 7, 0), high)
            merged = jnp.where(lane_even, own, pltpu.roll(other, 1, 1))
            for part in range(4):
                send_ref[part % 2, 2 * group + part // 2, q] = merged[2 * part : 2 * part + 2]


def unpack_blocks(half, i, recv_ref, slots_ref):
    row_low = lax.broadcasted_iota(jnp.int32, (8, 128), 0) % 2 == 0
    tiles = [
        jnp.concatenate([recv_ref[half, 8 * segment + i, q] for segment in range(4)], axis=0)
        for q in range(5)
    ]
    down = [pltpu.roll(value, 1, 0) for value in tiles]
    up = [pltpu.roll(value, 7, 0) for value in tiles]
    count = jnp.where(row_low, up[4], tiles[4])
    kept = jnp.where(row_low, count, 9.0 - count)
    for k in range(8):
        if k % 2 == 0:
            value = jnp.where(row_low, tiles[k // 2], down[(8 - k) // 2])
        else:
            value = jnp.where(row_low, up[k // 2], tiles[(7 - k) // 2])
        if k > 0:
            value = jnp.where(kept > k, value, 0.0)
        slots_ref[i, k] = value


def shade(density, state, sample_count):
    opacity, red, green, blue = state
    u = jnp.exp2(density)
    third = u * (LOG2E - u * (LOG2E / 2 - u * (LOG2E / 3)))
    soft = jnp.where(u < 2.0**-8, third, jnp.log2(1.0 + u))
    t = 1.5 * math.log(2.0) / sample_count
    alpha = soft * (t - soft * (t**2 / 2 - soft * (t**3 / 6 - soft * (t**4 / 24))))
    weight = (1.0 - opacity) * alpha
    v = jnp.exp2(0.5 * density - 1.5 * LOG2E)
    red = red + weight * jnp.exp2(density - soft)
    green = green + weight * jnp.exp2(density * density * (-1.0 / (4 * LOG2E)))
    blue = blue + weight * jnp.exp2(-jnp.log2(1.0 + v))
    return opacity + weight, red, green, blue


def render(x, flip, slots_ref, picture_ref, sample_count):
    unit = 2 * LOG2E
    c0 = cosine(0, 0)
    b1x, b2x = cosine(1, x), cosine(2, x)
    p, q, h = cosine(1, 0), cosine(1, 1), cosine(2, 0)
    turn = (1 - 2 * flip).astype(jnp.float32)

    def step(i, states):
        at = i + flip * (7 - 2 * i)
        a = [slots_ref[at, k] for k in range(8)]
        base = (unit * c0**3) * a[0] + (unit * c0**2 * b1x) * a[2] + (unit * c0**2 * b2x) * a[6]
        along = (unit * c0**2) * a[1] + (unit * c0 * b1x) * a[5]
        curve = (unit * c0**2 * h) * a[4]
        deep, tilt = (unit * c0**2 * turn) * a[3], (unit * c0 * turn) * a[7]
        outer, inner = base + curve, base - curve
        plane = [outer + p * along, inner + q * along, inner - q * along, outer - p * along]
        slope = [deep + p * tilt, deep + q * tilt, deep - q * tilt, deep - p * tilt]
        result = []
        for y in range(4):
            state = states[y]
            far, near = p * slope[y], q * slope[y]
            for density in (plane[y] + far, plane[y] + near, plane[y] - near, plane[y] - far):
                state = shade(density, state, sample_count)
            result.append(state)
        return tuple(result)

    zero = jnp.zeros((8, 128), jnp.float32)
    states = lax.fori_loop(0, 8, step, tuple((zero,) * 4 for _ in range(4)), unroll=UNROLL)
    for y in range(4):
        opacity, red, green, blue = states[y]
        values = [red, green, blue, opacity]
        for distance in (2, 4):
            clear = 1.0 - values[3]
            if distance == 2:
                beyond = [
                    jnp.where(flip > 0, pltpu.roll(value, 2, 0), pltpu.roll(value, 6, 0))
                    for value in values
                ]
            else:
                beyond = [pltpu.roll(value, 4, 0) for value in values]
            values = [value + clear * more for value, more in zip(values, beyond)]
        for channel, value in enumerate(values):
            value = jnp.where(flip > 0, pltpu.roll(value, 2, 0), value)
            start = channel * 32 + x * 8 + y * 2
            picture_ref[start : start + 2, :] = value[0:2]


def kernel(
    sample_count,
    tiles,
    depths,
    coef_hbm,
    keep_hbm,
    flip_ref,
    out_ref,
    coef_ref,
    keep_ref,
    coef_sem,
    keep_sem,
    send_ref,
    recv_ref,
    slots_ref,
    picture_ref,
    ordered_ref,
    send2_ref,
    recv2_first,
    recv2_second,
    send_sem,
    recv_sem,
    send2_sem,
    recv2_sem,
):
    loads = [
        pltpu.make_async_copy(coef_hbm, coef_ref, coef_sem),
        pltpu.make_async_copy(keep_hbm, keep_ref, keep_sem),
    ]
    for load in loads:
        load.start()
    tile = lax.axis_index("tile")
    depth = lax.axis_index("depth")
    recv2 = (recv2_first, recv2_second)

    xs = [lax.rem(lax.div(tile, 8) + k, 4) * 8 for k in range(4)]
    ys = [lax.rem(lax.rem(tile, 8) + k, 8) for k in range(8)]
    steps = [(dx, dy) for dx in range(4) for dy in range(8)][1:]
    steps.sort(key=lambda step: -min(step[0], 4 - step[0]) - min(step[1], 8 - step[1]))
    peers = [xs[dx] + ys[dy] for dx, dy in steps]
    bands = [lax.rem(depth + k, depths) for k in (8, 7, 9, 6, 10, 5, 11, 4, 12, 3, 13, 2, 14, 1, 15)]

    barrier = pltpu.get_barrier_semaphore()
    for to in peers:
        pl.semaphore_signal(barrier, inc=1, device_id=(to, depth), device_id_type=MESH)
    for to in bands:
        pl.semaphore_signal(barrier, inc=1, device_id=(tile, to), device_id_type=MESH)
    for load in loads:
        load.wait()
    pack_strips(coef_ref, keep_ref, send_ref)
    pl.semaphore_wait(barrier, tiles + depths - 2)

    def strip_copy(half, to, source):
        return pltpu.make_async_remote_copy(
            src_ref=send_ref.at[half, to],
            dst_ref=recv_ref.at[half, source],
            send_sem=send_sem.at[half, to],
            recv_sem=recv_sem.at[half, source],
            device_id=(to, depth),
            device_id_type=MESH,
        )

    def band_copy(half, to, source):
        return pltpu.make_async_remote_copy(
            src_ref=send2_ref.at[half, to],
            dst_ref=recv2[half].at[source],
            send_sem=send2_sem.at[half, to],
            recv_sem=recv2_sem.at[half, source],
            device_id=(tile, to),
            device_id_type=MESH,
        )

    for half in range(2):
        for to in peers:
            strip_copy(half, to, tile).start()
        recv_ref[half, tile] = send_ref[half, tile]

    flip = flip_ref[0]
    for half in range(2):
        for source in peers:
            strip_copy(half, source, source).wait_recv()

        def unpack_step(i, carry):
            unpack_blocks(half, i, recv_ref, slots_ref)
            return carry

        lax.fori_loop(0, 8, unpack_step, 0)
        for x in range(4):
            render(x, flip, slots_ref, picture_ref, sample_count)
        for channel in range(4):
            for x in range(4):
                for block in range(2):
                    source = channel * 32 + x * 8 + block
                    start = channel * 32 + (3 - x) * 8 + block * 4
                    ordered_ref[start : start + 4, :] = picture_ref[pl.ds(source, 4, stride=2), :]
        turned = ordered_ref[...].T
        for band in range(16):
            send2_ref[half, band] = turned[8 * band : 8 * band + 8]
        for to in bands:
            band_copy(half, to, depth).start()
        recv2[half][depth] = send2_ref[half, depth]

    for half in range(2):
        for to in peers:
            strip_copy(half, to, tile).wait_send()
    lane = lax.broadcasted_iota(jnp.int32, (8, 128), 1)
    row_first = lax.broadcasted_iota(jnp.int32, (8, 128), 0) < 4
    for half in range(2):
        for source in bands:
            band_copy(half, source, source).wait_recv()
        passing = jnp.ones((8, 128), jnp.float32)
        total = jnp.zeros((8, 128), jnp.float32)
        for brick in range(16):
            front = recv2[half][brick + flip * (15 - 2 * brick)]
            opacity = jnp.where(lane >= 96, front, pltpu.roll(front, 64, 1))
            opacity = jnp.where(lane // 32 % 2 == 1, opacity, pltpu.roll(opacity, 32, 1))
            total = total + passing * front
            passing = passing * (1.0 - opacity)
        for channel in range(4):
            value = jnp.zeros((8, 128), jnp.float32)
            for pair in range(4):
                shift = 8 * pair - 32 * channel - 24
                first = pltpu.roll(total, shift % 128, 1)[2 * pair : 2 * pair + 1]
                second = pltpu.roll(total, (shift - 32) % 128, 1)[2 * pair + 1 : 2 * pair + 2]
                rows = jnp.where(
                    row_first, jnp.broadcast_to(first, (8, 128)), jnp.broadcast_to(second, (8, 128))
                )
                spread = pltpu.roll(rows, 0, 1, stride=8, stride_axis=0)
                value = jnp.where(lane // 8 == pair, spread, value)
            out_ref[channel, 8 * half : 8 * half + 8, :] = value[:, :32]
    for half in range(2):
        for to in bands:
            band_copy(half, to, depth).wait_send()


def per_device(coefficients, keep_count, view_flip):
    tiles, depths = lax.axis_size("tile"), lax.axis_size("depth")
    sample_count = 4 * tiles * depths
    whole = pl.BlockSpec(memory_space=pltpu.VMEM)
    far = pl.BlockSpec(memory_space=pltpu.HBM)
    return pl.pallas_call(
        functools.partial(kernel, sample_count, tiles, depths),
        out_shape=jax.ShapeDtypeStruct((4, 16, 32), jnp.float32),
        in_specs=[far, far, pl.BlockSpec(memory_space=pltpu.SMEM)],
        out_specs=whole,
        scratch_shapes=[
            pltpu.VMEM((8, 128, 128), jnp.float32),
            pltpu.VMEM((128, 128), jnp.int32),
            pltpu.SemaphoreType.DMA,
            pltpu.SemaphoreType.DMA,
            pltpu.VMEM((2, 32, 5, 2, 128), jnp.float32),
            pltpu.VMEM((2, 32, 5, 2, 128), jnp.float32),
            pltpu.VMEM((8, 8, 8, 128), jnp.float32),
            pltpu.VMEM((128, 128), jnp.float32),
            pltpu.VMEM((128, 128), jnp.float32),
            pltpu.VMEM((2, 16, 8, 128), jnp.float32),
            pltpu.VMEM((16, 8, 128), jnp.float32),
            pltpu.VMEM((16, 8, 128), jnp.float32),
            pltpu.SemaphoreType.DMA((2, 32)),
            pltpu.SemaphoreType.DMA((2, 32)),
            pltpu.SemaphoreType.DMA((2, 16)),
            pltpu.SemaphoreType.DMA((2, 16)),
        ],
        compiler_params=pltpu.CompilerParams(collective_id=0, has_side_effects=True),
    )(coefficients.reshape(8, 128, 128), keep_count.reshape(128, 128), view_flip)


def solution(mesh):
    placed = (P(None, "depth", "tile", None, None), P("depth", "tile", None, None), P("tile"))
    return jax.shard_map(
        per_device, mesh=mesh, in_specs=placed, out_specs=P(None, "tile", "depth"), check_vma=False
    )
```
